32 devices in a mesh: section: 2 (over core), dp: 16 (over z, y, x).
Axes of the slice: x: 2, y: 2, z: 4, core: 2. Of those that a mesh axis runs over, the one named last changes fastest.
Arguments:
- tokens: bfloat16 [4096, 768], P('dp'), may hold values from -6 to 6
- cotangent: bfloat16 [4096, 768], P('dp'), may hold values from -6 to 6
- lengths: int32 [16, 2, 3], P('dp'), may hold values from 1 to 96, 128 in all within a row
- norm_gain: bfloat16 [2, 768], P('section', 'dp'), may hold values from 0.099609375 to 1.8984375
- in_weight: bfloat16 [2, 768, 3352], P('section', 'dp'), may hold values from -0.21875 to 0.21875
- filter_weight: bfloat16 [2, 4, 1792], P('section', None, 'dp'), may hold values from -3 to 3
- filter_bias: bfloat16 [2, 1792], P('section', 'dp'), may hold values from -3 to 3
- step_bias: bfloat16 [2, 24], P('section'), may hold values from -5 to -1.5
- decay_log: bfloat16 [2, 24], P('section'), may hold values from 0 to 2.765625
- skip_gain: bfloat16 [2, 24], P('section'), may hold values from 0.5 to 1.5
- mix_gain: bfloat16 [2, 1536], P('section', 'dp'), may hold values from 0.099609375 to 1.8984375
- out_weight: bfloat16 [2, 1536, 768], P('section', 'dp'), may hold values from -0.15625 to 0.15625
Outputs:
- section_outputs: bfloat16 [2, 4096, 768], P('section', 'dp')
- input_grads: bfloat16 [2, 4096, 768], P('section', 'dp')
- norm_gain_grad: float32 [2, 768], P('section', 'dp')
- in_weight_grad: float32 [2, 768, 3352], P('section', 'dp')
- filter_weight_grad: float32 [2, 4, 1792], P('section', None, 'dp')
- filter_bias_grad: float32 [2, 1792], P('section', 'dp')
- step_bias_grad: float32 [2, 24], P('section')
- decay_log_grad: float32 [2, 24], P('section')
- skip_gain_grad: float32 [2, 24], P('section')
- mix_gain_grad: float32 [2, 1536], P('section', 'dp')
- out_weight_grad: float32 [2, 1536, 768], P('section', 'dp')
The draws below stay inside these ranges and needn't reach their ends.
Inputs may be any that keep to these rules, and one draw needn't show every extreme that they name: Each micro-batch of each device holds 3 sequences whose lengths sum to 128; the longest is exactly 96.
All inputs are finite; a program needn't handle non-finite values.
Results may differ from the reference program's by a relative error of at most 0.01.
Values may be sent and summed in bfloat16 or wider, within the bound.
No kernel may reach another device: no remote copies, remote signals or barrier semaphores. Data moves between devices by JAX's collectives and lax.ppermute only.
A program may use at most 128 MiB of HBM per device.

```python
import math
from functools import partial
import jax
import jax.numpy as jnp
import numpy as np
from jax import lax

D = 768
HEADS = 24
CONV = 4
GROUP = 128
MB = 2
NSEQ = 3
SEQ_MAX = 96
INNER = 1536
CONV_CH = 1792
PROJ = 3352
TOKENS = 4096
N_DP = 16


def block_scale(stream_key, dims, split, low, top_value):
    level = 1.0
    for axis_at, shards_of in split:
        heights = jax.random.uniform(jax.random.fold_in(jax.random.fold_in(stream_key, 6), axis_at), (shards_of,), jnp.float32, low / len(split), top_value / len(split))
        level = level * jnp.repeat(jnp.exp(heights), dims[axis_at] // shards_of).reshape((-1,) + (1,) * (len(dims) - 1 - axis_at))
    return level


def split_up(count, total, limit, skew):
    loads = [(1 << 20) // math.isqrt(grade ** skew) + 1 for grade in range(2, count + 1)]
    surplus, given = total - limit - (count - 1), [1] * (count - 1)
    while surplus > 0:
        candidates = [i for i in range(count - 1) if given[i] < limit]
        whole, budget = sum([loads[i] for i in candidates]), surplus
        for i in candidates:
            extra = min(limit - given[i], max(1, budget * loads[i] // whole), surplus)
            given[i] = given[i] + extra
            surplus = surplus - extra
    return np.array([limit] + given)


def ragged_sizes(own_key, number_of, total, bound, slope):
    if number_of == 2:
        one = jax.random.randint(own_key, (), max(1, total - bound), min(bound, total - 1) + 1)
        return jnp.stack([one, total - one])
    tallies = jnp.asarray(split_up(number_of, total, bound, slope), jnp.int32)
    couples = (number_of - 1) // 2
    giver, sink = tallies[1:1 + 2 * couples:2], tallies[2:2 + 2 * couples:2]
    margin = jnp.minimum(giver - 1, bound - sink)
    passed = jax.random.randint(jax.random.fold_in(own_key, 1), (couples,), 0, 1 << 20) % (margin + 1)
    tallies = tallies.at[1:1 + 2 * couples:2].set(giver - passed).at[2:2 + 2 * couples:2].set(sink + passed)
    return tallies[jax.random.permutation(jax.random.fold_in(own_key, 2), number_of)]


def noise(stream_key, dims, scale, most, pieces=(), kind=jnp.bfloat16):
    array = scale * jax.random.normal(stream_key, dims, jnp.float32)
    if pieces:
        array = array * block_scale(stream_key, dims, pieces, -0.22, 0.18)
    return jnp.clip(array, -most, most).astype(kind)


def setup_inputs(seed: int = 0) -> dict:
    key_of = jax.random.split(jax.random.key(seed), 13)
    tokens = noise(key_of[0], (TOKENS, D), 1.0, 6.0, ((0, 16),))
    cotangent = noise(key_of[1], (TOKENS, D), 1.0, 6.0, ((0, 16),))
    lengths = jax.vmap(lambda own: ragged_sizes(own, NSEQ, GROUP, SEQ_MAX, 2))(jax.random.split(key_of[2], N_DP * MB)).reshape((N_DP, MB, NSEQ)).astype(jnp.int32)
    norm_gain = jnp.clip(1.0 + 0.18 * jax.random.normal(key_of[3], (2, D), jnp.float32), 0.099609375, 1.8984375).astype(jnp.bfloat16)
    in_weight = noise(key_of[4], (2, D, PROJ), D ** -0.5, 0.21875, ((0, 2), (1, 16)))
    filter_weight = noise(key_of[5], (2, CONV, CONV_CH), CONV ** -0.5, 3.0, ((0, 2), (2, 16)))
    filter_bias = noise(key_of[6], (2, CONV_CH), 0.5, 3.0, ((0, 2), (1, 16)))
    step_bias = jnp.clip(-5.0 + 3.5 * jax.random.uniform(key_of[7], (2, HEADS), jnp.float32) ** block_scale(key_of[7], (2, HEADS), ((0, 2),), -0.2, 0.2), -5.0, -1.5).astype(jnp.bfloat16)
    decay_log = jnp.clip(2.765625 * jax.random.uniform(key_of[8], (2, HEADS), jnp.float32) ** block_scale(key_of[8], (2, HEADS), ((0, 2),), -0.2, 0.2), 0.0, 2.765625).astype(jnp.bfloat16)
    skip_gain = jnp.clip(0.5 + 1.0 * jax.random.uniform(key_of[9], (2, HEADS), jnp.float32) ** block_scale(key_of[9], (2, HEADS), ((0, 2),), -0.2, 0.2), 0.5, 1.5).astype(jnp.bfloat16)
    mix_gain = jnp.clip(1.0 + 0.18 * jax.random.normal(key_of[10], (2, INNER), jnp.float32), 0.099609375, 1.8984375).astype(jnp.bfloat16)
    out_weight = noise(key_of[11], (2, INNER, D), INNER ** -0.5, 0.15625, ((0, 2), (1, 16)))
    return dict(tokens=tokens, cotangent=cotangent, lengths=lengths, norm_gain=norm_gain, in_weight=in_weight, filter_weight=filter_weight, filter_bias=filter_bias, step_bias=step_bias, decay_log=decay_log, skip_gain=skip_gain, mix_gain=mix_gain, out_weight=out_weight)


@jax.custom_vjp
def low(v):
    return lax.optimization_barrier(v.astype(jnp.bfloat16)).astype(jnp.float32)

@jax.custom_vjp
def low_back(v):
    return v

def low_keep(v):
    return (low(v), None)

def low_pass(kept, grad):
    return (grad,)

def back_keep(v):
    return (v, None)

def back_low(kept, grad):
    return (low(grad),)
low.defvjp(low_keep, low_pass)
low_back.defvjp(back_keep, back_low)
highest = lax.Precision.HIGHEST
eps_value = 1e-05

def rms_scale(values, gain):
    return values * lax.rsqrt(lax.optimization_barrier(jnp.mean(values * values, axis=-1, keepdims=True)) + eps_value) * gain

def segment_ids(seq_lengths, group_rows):
    finish = jnp.cumsum(seq_lengths)
    places = jnp.arange(group_rows, dtype=jnp.int32)
    return lax.optimization_barrier(jnp.sum((places[:, None] >= finish[None, :]).astype(jnp.int32), axis=1))

def mix_block(gate_part, signal_part, raw_step, seg_ids, filter_taps, filter_shift, step_shift, decay_rates, skip_scale, mix_scale):
    row_count, inner_width = gate_part.shape
    head_count = raw_step.shape[1]
    head_width = inner_width // head_count
    state_width = (signal_part.shape[1] - inner_width) // 2
    kernel_width = filter_taps.shape[0]
    padded = jnp.pad(signal_part, ((kernel_width - 1, 0), (0, 0)))
    seg_padded = jnp.pad(seg_ids, (kernel_width - 1, 0), constant_values=-1)
    filtered = jnp.zeros_like(signal_part) + filter_shift
    for offset in range(kernel_width):
        same_seq = (seg_padded[offset:offset + row_count] == seg_ids)[:, None]
        filtered = filtered + jnp.where(same_seq, padded[offset:offset + row_count], 0.0) * filter_taps[offset]
    filtered = jax.nn.silu(filtered)
    values = filtered[:, :inner_width]
    key_part = filtered[:, inner_width:inner_width + state_width]
    query_part = filtered[:, inner_width + state_width:]
    step_size = jax.nn.softplus(raw_step + step_shift)
    log_decay = jnp.cumsum(step_size * -jnp.exp(decay_rates), axis=0).T
    places = jnp.arange(row_count)
    allowed = ((seg_ids[:, None] == seg_ids[None, :]) & (places[:, None] >= places[None, :]))[None]
    spread_log = log_decay[:, :, None] - log_decay[:, None, :]
    decay_matrix = jnp.where(allowed, jnp.exp(jnp.where(allowed, spread_log, 0.0)), 0.0)
    key_query = jnp.dot(query_part, key_part.T, precision=highest)
    mixing = decay_matrix * key_query[None] * step_size.T[:, None, :]
    head_values = values.reshape(row_count, head_count, head_width)
    result = jnp.einsum('hts,shp->thp', mixing, head_values, precision=highest)
    result = result + skip_scale[None, :, None] * head_values
    gated_rows = result.reshape(row_count, inner_width) * jax.nn.silu(gate_part)
    return rms_scale(gated_rows, mix_scale)

def block_one(resid, seg_ids, params):
    block_gain, in_full, filter_full, bias_full, step_shift, decay_rates, skip_scale, mix_scale, out_full = params
    normed = low(rms_scale(resid, block_gain))
    projected = low_back(jnp.dot(normed, in_full, precision=highest))
    mixed = low(mix_block(projected[:, :INNER], projected[:, INNER:INNER + CONV_CH], projected[:, INNER + CONV_CH:], seg_ids, filter_full, bias_full, step_shift, decay_rates, skip_scale, mix_scale))
    return resid + low_back(jnp.dot(mixed, out_full, precision=highest))

def reference(tokens, cotangent, lengths, norm_gain, in_weight, filter_weight, filter_bias, step_bias, decay_log, skip_gain, mix_gain, out_weight):
    first_input = tokens.astype(jnp.float32).reshape(N_DP, MB, GROUP, D)
    cot_input = cotangent.astype(jnp.float32).reshape(N_DP, MB, GROUP, D)
    seg_all = jax.vmap(jax.vmap(partial(segment_ids, group_rows=GROUP)))(lengths)
    weights = (norm_gain, in_weight, filter_weight, filter_bias, step_bias, decay_log, skip_gain, mix_gain, out_weight)
    params_zero = tuple((weight[0].astype(jnp.float32) for weight in weights))
    params_one = tuple((weight[1].astype(jnp.float32) for weight in weights))

    def device_pass(carry, inputs):
        resid_rows, cot_rows, seg_rows = inputs

        def first_section(resid_all, params):
            return low(low_back(jax.vmap(block_one, in_axes=(0, 0, None))(resid_all, seg_rows, params)))

        def second_section(resid_all, params):
            return jax.vmap(block_one, in_axes=(0, 0, None))(resid_all, seg_rows, params)
        middle, first_back = jax.vjp(first_section, resid_rows, params_zero)
        final, second_back = jax.vjp(second_section, middle, params_one)
        middle_grad, second_grads = second_back(cot_rows)
        input_grad, first_grads = first_back(middle_grad)
        new_carry = []
        for section_number, grads in ((0, first_grads), (1, second_grads)):
            members = []
            for number in range(9):
                members.append(carry[section_number][number] + grads[number])
            new_carry.append(tuple(members))
        outputs = (middle.astype(jnp.bfloat16), final.astype(jnp.bfloat16), input_grad.astype(jnp.bfloat16), middle_grad.astype(jnp.bfloat16))
        return ((new_carry[0], new_carry[1]), outputs)
    start = tuple((tuple((jnp.zeros(weight.shape[1:], jnp.float32) for weight in weights)) for section_number in range(2)))
    totals, outputs = lax.scan(device_pass, start, (first_input, cot_input, seg_all))
    middle_all, final_all, input_all, middle_grad_all = outputs
    section_outputs = jnp.stack([middle_all.reshape(TOKENS, D), final_all.reshape(TOKENS, D)])
    input_grads = jnp.stack([input_all.reshape(TOKENS, D), middle_grad_all.reshape(TOKENS, D)])
    stacked = [jnp.stack([totals[0][number], totals[1][number]]) for number in range(9)]
    return (section_outputs, input_grads, stacked[0], stacked[1], stacked[2], stacked[3], stacked[4], stacked[5], stacked[6], stacked[7], stacked[8])
```

```python
import functools

import jax
import jax.numpy as jnp
from jax import lax
from jax.sharding import PartitionSpec as P

D = 768
HEADS = 24
CONV = 4
GROUP = 128
MB = 2
INNER = 1536
CONV_CH = 1792
PROJ = 3352
STATE = 128
HEAD = 64

BLOCKS = 16
ROWS = D // BLOCKS
CUT = 1664
PACK = 2560
OUT_AT = (CUT, PACK - D)

both = ("section", "dp")
bf16 = jnp.bfloat16
f32 = jnp.float32
highest = lax.Precision.HIGHEST
eps_value = 1e-05


def dp_digits(mesh):
    count = mesh.shape["dp"]
    try:
        coords = [tuple(device.coords) for device in mesh.devices.reshape(2, count)[0]]
    except AttributeError:
        coords = [(i % 2, i // 2 % 2, i // 4) for i in range(count)]
    digits = []
    for axis in range(3):
        size = len({c[axis] for c in coords})
        if size > 1:
            digits.append((min(i for i in range(count) if coords[i][axis] != coords[0][axis]), size))
    digits.sort(key=lambda digit: (-digit[1], digit[0]))
    if count != BLOCKS or [size for _, size in digits] != [4, 2, 2]:
        return None
    return tuple(digits)


def swap_by(value, masks):
    count = lax.axis_size("dp")
    pairs = [(s * count + d, s * count + (d ^ masks[s])) for s in range(2) for d in range(count)]
    return lax.ppermute(value, both, pairs)


def swap_core(value):
    return lax.ppermute(value, "section", [(0, 1), (1, 0)])


def sum_all(value, digits):
    value = value + swap_core(value)
    for stride, size in digits:
        step = 1
        while step < size:
            value = value + swap_by(value, (stride * step,) * 2)
            step *= 2
    return value


def masks_of(digits):
    z, first, second = digits
    return tuple(
        tuple(kz * z[0] ^ k1 * a[0] ^ k2 * b[0] for k2 in range(2) for k1 in range(2) for kz in range(4))
        for a, b in ((first, second), (second, first))
    )


def gather_half(start, digits):
    z, first, second = digits
    stack = jnp.stack([start] + [swap_by(start, (k * z[0],) * 2) for k in range(1, 4)])
    stack = jnp.concatenate([stack, swap_by(stack, (first[0], second[0]))])
    return stack, swap_by(stack, (second[0], first[0]))


def scatter_half(kept, sent, digits):
    z, first, second = digits
    total = kept.astype(f32) + swap_core(sent).astype(f32)
    total = total.astype(bf16)
    total = (total[:8].astype(f32) + swap_by(total[8:], (second[0], first[0])).astype(f32)).astype(bf16)
    total = (total[:4].astype(f32) + swap_by(total[4:], (first[0], second[0])).astype(f32)).astype(bf16)
    done = total[0].astype(f32)
    for k in range(1, 4):
        done = done + swap_by(total[k], (k * z[0],) * 2).astype(f32)
    return done


def pack_halves(in_block, out_block):
    lead = in_block.shape[:-2]
    upper, lower = out_block[..., :ROWS, :], out_block[..., ROWS:, :]
    half = D // 2
    pad = lambda n: jnp.zeros(lead + (ROWS, n), in_block.dtype)
    first = [in_block[..., :CUT], upper[..., :half], lower[..., :half], pad(PACK - CUT - D)]
    second = [in_block[..., CUT:], pad(PACK - D - (PROJ - CUT)), upper[..., half:], lower[..., half:]]
    return jnp.concatenate(first, -1), jnp.concatenate(second, -1)


def unpack_halves(first, second):
    half = D // 2
    in_block = jnp.concatenate([first[..., :CUT], second[..., : PROJ - CUT]], -1)
    a, b = first[..., OUT_AT[0] : OUT_AT[0] + D], second[..., OUT_AT[1] : OUT_AT[1] + D]
    upper = jnp.concatenate([a[..., :half], b[..., :half]], -1)
    lower = jnp.concatenate([a[..., half:], b[..., half:]], -1)
    return in_block, jnp.concatenate([upper, lower], -2)


SMALL = ((D,), (CONV, CONV_CH), (CONV_CH,), (INNER,), (HEADS,), (HEADS,), (HEADS,))
SMALL_SIZE = 11392


def pack_small(parts):
    flat = jnp.concatenate([part.reshape(-1) for part in parts])
    return jnp.pad(flat, (0, SMALL_SIZE - flat.shape[0]))


def unpack_small(flat):
    parts, at = [], 0
    for shape in SMALL:
        size = 1
        for dim in shape:
            size *= dim
        parts.append(flat[at : at + size].reshape(shape))
        at += size
    return parts


def place_small(shards, me):
    parts = []
    for shape, shard in zip(SMALL, shards):
        if shape == (HEADS,):
            parts.append(jnp.where(me == 0, shard, jnp.zeros_like(shard)))
        else:
            at = (0,) * (len(shape) - 1) + (me * shard.shape[-1],)
            parts.append(lax.dynamic_update_slice(jnp.zeros(shape, shard.dtype), shard, at))
    return pack_small(parts)


def rms_scale(values, gain):
    return values * lax.rsqrt(jnp.mean(values * values, axis=-1, keepdims=True) + eps_value) * gain


def segment_ids(seq_lengths, group_rows):
    finish = jnp.cumsum(seq_lengths)
    places = jnp.arange(group_rows, dtype=jnp.int32)
    return jnp.sum((places[:, None] >= finish[None, :]).astype(jnp.int32), axis=1)


row_dims = (((0,), (0,)), ((), ()))
col_dims = (((1,), (1,)), ((), ()))

def mix_block(
    gate_part,
    signal_part,
    raw_step,
    seg_ids,
    filter_taps,
    filter_shift,
    step_shift,
    decay_rates,
    skip_scale,
    mix_scale,
):
    row_count, inner_width = gate_part.shape
    head_count = raw_step.shape[1]
    head_width = inner_width // head_count
    state_width = (signal_part.shape[1] - inner_width) // 2
    kernel_width = filter_taps.shape[0]
    padded = jnp.pad(signal_part, ((kernel_width - 1, 0), (0, 0)))
    seg_padded = jnp.pad(seg_ids, (kernel_width - 1, 0), constant_values=-1)
    filtered = jnp.zeros_like(signal_part) + filter_shift
    for offset in range(kernel_width):
        same_seq = (seg_padded[offset : offset + row_count] == seg_ids)[:, None]
        filtered = (
            filtered
            + jnp.where(same_seq, padded[offset : offset + row_count], 0.0) * filter_taps[offset]
        )
    filtered = jax.nn.silu(filtered)
    values = filtered[:, :inner_width]
    key_part = filtered[:, inner_width : inner_width + state_width]
    query_part = filtered[:, inner_width + state_width :]
    step_size = jax.nn.softplus(raw_step + step_shift)
    log_decay = jnp.cumsum(step_size * -jnp.exp(decay_rates), axis=0).T
    places = jnp.arange(row_count)
    allowed = ((seg_ids[:, None] == seg_ids[None, :]) & (places[:, None] >= places[None, :]))[None]
    spread_log = log_decay[:, :, None] - log_decay[:, None, :]
    decay_matrix = jnp.where(allowed, jnp.exp(jnp.where(allowed, spread_log, 0.0)), 0.0)
    key_query = jnp.dot(query_part, key_part.T, precision=highest)
    mixing = decay_matrix * key_query[None] * step_size.T[:, None, :]
    head_values = values.reshape(row_count, head_count, head_width)
    result = jnp.einsum("hts,shp->thp", mixing, head_values, precision=highest)
    result = result + skip_scale[None, :, None] * head_values
    gated_rows = result.reshape(row_count, inner_width) * jax.nn.silu(gate_part)
    return rms_scale(gated_rows, mix_scale)


def forward_one(resid, seg_ids, in_full, out_full, small):
    block_gain, taps, shift, mix_scale, step_shift, decay, skip = small
    normed = rms_scale(resid, block_gain).astype(bf16)
    projected = jnp.dot(normed, in_full, preferred_element_type=f32)
    mixed = mix_block(
        projected[:, :INNER], projected[:, INNER : INNER + CONV_CH], projected[:, INNER + CONV_CH :],
        seg_ids, taps, shift, step_shift, decay, skip, mix_scale,
    ).astype(bf16)
    output = resid + jnp.dot(mixed, out_full, preferred_element_type=f32)
    return output.astype(bf16), normed, projected, mixed


def backward_one(grad_output, resid, normed, projected, mixed, seg_ids, in_full, out_full, small):
    block_gain, taps, shift, mix_scale, step_shift, decay, skip = small
    grad_mixed = lax.dot_general(grad_output, out_full, col_dims, preferred_element_type=f32)
    mixer = lambda gate, signal, raw, *rest: mix_block(gate, signal, raw, seg_ids, *rest)
    _, mixer_back = jax.vjp(
        mixer, projected[:, :INNER], projected[:, INNER : INNER + CONV_CH], projected[:, INNER + CONV_CH :],
        taps, shift, step_shift, decay, skip, mix_scale,
    )
    grads = mixer_back(grad_mixed)
    grad_projected = jnp.concatenate(grads[:3], axis=1).astype(bf16)
    grad_normed = lax.dot_general(grad_projected, in_full, col_dims, preferred_element_type=f32)
    _, norm_back = jax.vjp(rms_scale, resid, block_gain)
    grad_resid, grad_gain = norm_back(grad_normed)
    grad_resid = (grad_resid + grad_output.astype(f32)).astype(bf16)
    grad_in = lax.dot_general(normed, grad_projected, row_dims, preferred_element_type=f32)
    grad_out = lax.dot_general(mixed, grad_output, row_dims, preferred_element_type=f32)
    return grad_resid, grad_in, grad_out, pack_small((grad_gain, grads[3], grads[4], grads[8], *grads[5:8]))


def on_device(digits, tokens, cotangent, lengths, norm_gain, in_weight, filter_weight, filter_bias,
              step_bias, decay_log, skip_gain, mix_gain, out_weight):
    core = lax.axis_index("section")
    me = lax.axis_index("dp")
    first_core = core == 0
    pick = lambda a, b: jnp.where(first_core, a, b)
    shards = tuple(a[0] for a in (norm_gain, filter_weight, filter_bias, mix_gain, step_bias, decay_log, skip_gain))

    if digits:
        own_small = place_small(shards, me)
        zero = jnp.zeros_like(own_small)
        small_all = sum_all(jnp.stack([pick(own_small, zero), pick(zero, own_small)]), digits)
        first, second = pack_halves(in_weight[0], out_weight[0])
        other = swap_core(pick(second, first))
        masks = masks_of(digits)
        weights = []
        for s, start in enumerate((pick(first, other), pick(other, second))):
            mine = jnp.concatenate(gather_half(start, digits))
            theirs = swap_core(mine)
            halves = []
            for h, stack in enumerate((pick(mine, theirs), pick(theirs, mine))):
                places = jnp.array([masks[h].index(r) for r in range(BLOCKS)])
                halves.append(jnp.take(stack, places[jnp.arange(BLOCKS) ^ me], axis=0))
            in_full, out_full = unpack_halves(*halves)
            weights.append((in_full.reshape(D, PROJ), out_full.reshape(INNER, D)))
    else:
        gather = lambda a, axis: lax.all_gather(
            lax.all_gather(a, "dp", axis=axis, tiled=True), "section", axis=0, tiled=True
        )
        in_all, out_all = gather(in_weight, 1), gather(out_weight, 1)
        weights = [(in_all[s], out_all[s]) for s in range(2)]
        parts = (gather(norm_gain, 1), gather(filter_weight, 2), gather(filter_bias, 1), gather(mix_gain, 1)) + tuple(
            lax.all_gather(a, "section", axis=0, tiled=True) for a in (step_bias, decay_log, skip_gain)
        )
        small_all = jnp.stack([pack_small([part[s] for part in parts]) for s in range(2)])

    smalls = [[p.astype(f32) for p in unpack_small(small_all[s])] for s in range(2)]
    rows = lambda a: lax.dynamic_slice_in_dim(a, core * GROUP, GROUP, 0)
    seg_ids = segment_ids(lax.dynamic_index_in_dim(lengths[0], core, 0, keepdims=False), GROUP)
    start = rows(tokens)
    middle, *kept_0 = forward_one(start.astype(f32), seg_ids, *weights[0], smalls[0])
    final, *kept_1 = forward_one(middle.astype(f32), seg_ids, *weights[1], smalls[1])
    grad_1, in_1, out_1, small_1 = backward_one(
        rows(cotangent), middle.astype(f32), *kept_1, seg_ids, *weights[1], smalls[1])
    grad_0, in_0, out_0, small_0 = backward_one(
        grad_1, start.astype(f32), *kept_0, seg_ids, *weights[0], smalls[0])

    def own_rows(for_0, for_1):
        other = swap_core(pick(for_1, for_0))
        own = pick(for_0, for_1)
        return jnp.concatenate([pick(own, other), pick(other, own)])[None]

    section_outputs = own_rows(middle, final)
    input_grads = own_rows(grad_0, grad_1)
    small_sum = jnp.stack([small_0, small_1])
    if digits:
        done = []
        for in_grad, out_grad in ((in_1, out_1), (in_0, out_0)):
            halves = pack_halves(in_grad.reshape(BLOCKS, ROWS, PROJ), out_grad.reshape(BLOCKS, 2 * ROWS, D))
            stacks = [
                jnp.take(half.astype(bf16), jnp.array(masks[h]) ^ me, axis=0) for h, half in enumerate(halves)
            ]
            done.append(scatter_half(pick(*stacks), pick(*stacks[::-1]), digits))
        done_1, done_0 = done
        other = swap_core(pick(done_1, done_0))
        own = pick(done_0, done_1)
        in_own, out_own = unpack_halves(pick(own, other), pick(other, own))
        small_sum = sum_all(small_sum, digits)
    else:
        scatter = lambda a: lax.psum_scatter(
            lax.psum_scatter(a, "section", scatter_dimension=0, tiled=True), "dp", scatter_dimension=1, tiled=True)[0]
        in_own, out_own = scatter(jnp.stack([in_0, in_1])), scatter(jnp.stack([out_0, out_1]))
        small_sum = lax.psum(small_sum, both)
    small_own = unpack_small(lax.dynamic_index_in_dim(small_sum, core, 0, keepdims=False))
    cut = []
    for part, shard in zip(small_own, shards):
        if shard.shape != part.shape:
            part = lax.dynamic_slice_in_dim(part, me * shard.shape[-1], shard.shape[-1], part.ndim - 1)
        cut.append(part[None])
    return (section_outputs, input_grads, cut[0], in_own[None], cut[1], cut[2], cut[4], cut[5], cut[6], cut[3],
            out_own[None])


def solution(mesh):
    placed = (
        P("dp", None), P("dp", None), P("dp", None, None), P("section", "dp"), P("section", "dp", None),
        P("section", None, "dp"), P("section", "dp"), P("section", None), P("section", None), P("section", None),
        P("section", "dp"), P("section", "dp", None),
    )
    return jax.shard_map(
        functools.partial(on_device, dp_digits(mesh)),
        mesh=mesh,
        in_specs=placed,
        out_specs=(
            P("section", "dp", None), P("section", "dp", None), P("section", "dp"), P("section", "dp", None),
            P("section", None, "dp"), P("section", "dp"), P("section", None), P("section", None),
            P("section", None), P("section", "dp"), P("section", "dp", None),
        ),
        check_vma=False,
    )
```

```python
import functools

import jax
import jax.numpy as jnp
from jax import lax
from jax.experimental import pallas as pl
from jax.experimental.pallas import tpu as pltpu
from jax.sharding import PartitionSpec as P

D = 768
HEADS = 24
CONV = 4
GROUP = 128
MB = 2
INNER = 1536
CONV_CH = 1792
PROJ = 3352
STATE = 128
HEAD = 64

BLOCKS = 16
ROWS = D // BLOCKS
CUT = 1664
PACK = 2560
OUT_AT = (CUT, PACK - D)

both = ("section", "dp")
bf16 = jnp.bfloat16
f32 = jnp.float32
highest = lax.Precision.HIGHEST
eps_value = 1e-05


def dp_digits(mesh):
    count = mesh.shape["dp"]
    try:
        coords = [tuple(device.coords) for device in mesh.devices.reshape(2, count)[0]]
    except AttributeError:
        coords = [(i % 2, i // 2 % 2, i // 4) for i in range(count)]
    digits = []
    for axis in range(3):
        size = len({c[axis] for c in coords})
        if size > 1:
            digits.append((min(i for i in range(count) if coords[i][axis] != coords[0][axis]), size))
    digits.sort(key=lambda digit: (-digit[1], digit[0]))
    if count != BLOCKS or [size for _, size in digits] != [4, 2, 2]:
        return None
    return tuple(digits)


def swap_by(value, masks):
    count = lax.axis_size("dp")
    pairs = [(s * count + d, s * count + (d ^ masks[s])) for s in range(2) for d in range(count)]
    return lax.ppermute(value, both, pairs)


def swap_core(value):
    return lax.ppermute(value, "section", [(0, 1), (1, 0)])


def sum_all(value, digits):
    value = value + swap_core(value)
    for stride, size in digits:
        step = 1
        while step < size:
            value = value + swap_by(value, (stride * step,) * 2)
            step *= 2
    return value


def masks_of(digits):
    z, first, second = digits
    return tuple(
        tuple(kz * z[0] ^ k1 * a[0] ^ k2 * b[0] for k2 in range(2) for k1 in range(2) for kz in range(4))
        for a, b in ((first, second), (second, first))
    )


def gather_half(start, digits):
    z, first, second = digits
    stack = jnp.stack([start] + [swap_by(start, (k * z[0],) * 2) for k in range(1, 4)])
    stack = jnp.concatenate([stack, swap_by(stack, (first[0], second[0]))])
    return stack, swap_by(stack, (second[0], first[0]))


def scatter_half(kept, sent, digits):
    z, first, second = digits
    total = kept.astype(f32) + swap_core(sent).astype(f32)
    total = total.astype(bf16)
    total = (total[:8].astype(f32) + swap_by(total[8:], (second[0], first[0])).astype(f32)).astype(bf16)
    total = (total[:4].astype(f32) + swap_by(total[4:], (first[0], second[0])).astype(f32)).astype(bf16)
    done = total[0].astype(f32)
    for k in range(1, 4):
        done = done + swap_by(total[k], (k * z[0],) * 2).astype(f32)
    return done


def pack_halves(in_block, out_block):
    lead = in_block.shape[:-2]
    upper, lower = out_block[..., :ROWS, :], out_block[..., ROWS:, :]
    half = D // 2
    pad = lambda n: jnp.zeros(lead + (ROWS, n), in_block.dtype)
    first = [in_block[..., :CUT], upper[..., :half], lower[..., :half], pad(PACK - CUT - D)]
    second = [in_block[..., CUT:], pad(PACK - D - (PROJ - CUT)), upper[..., half:], lower[..., half:]]
    return jnp.concatenate(first, -1), jnp.concatenate(second, -1)


def unpack_halves(first, second):
    half = D // 2
    in_block = jnp.concatenate([first[..., :CUT], second[..., : PROJ - CUT]], -1)
    a, b = first[..., OUT_AT[0] : OUT_AT[0] + D], second[..., OUT_AT[1] : OUT_AT[1] + D]
    upper = jnp.concatenate([a[..., :half], b[..., :half]], -1)
    lower = jnp.concatenate([a[..., half:], b[..., half:]], -1)
    return in_block, jnp.concatenate([upper, lower], -2)


WIDE = 3456
RAW_AT = INNER + CONV_CH
LANES = 128
PAIRS = HEADS // 2
GAIN_AT, TAPS_AT, SHIFT_AT, MIX_AT = 0, D, D + CONV * CONV_CH, D + (CONV + 1) * CONV_CH
STEP_AT = MIX_AT + INNER
DECAY_AT, SKIP_AT = STEP_AT + LANES, STEP_AT + 2 * LANES
SMALL_SIZE = SKIP_AT + LANES
SMALL = (
    (GAIN_AT, (D,)),
    (TAPS_AT, (CONV, CONV_CH)),
    (SHIFT_AT, (CONV_CH,)),
    (MIX_AT, (INNER,)),
    (STEP_AT, (HEADS,)),
    (DECAY_AT, (HEADS,)),
    (SKIP_AT, (HEADS,)),
)
nt_dims = (((1,), (1,)), ((), ()))


def chunk(j):
    return pl.ds(pl.multiple_of(j * LANES, LANES), LANES)


def sigmoid(v):
    return 1.0 / (1.0 + jnp.exp(-v))


def exact_dot(a, b, dims=(((1,), (0,)), ((), ()))):
    return lax.dot_general(a, b, dims, precision=highest, preferred_element_type=f32)


def start_weights(digits, ids, stacks, win, wout, sems):
    z, first, second = digits
    me, core = ids[0], ids[1]
    half = D // 2
    for owner in range(2):

        @pl.when(core == owner)
        def _():
            for h in range(2):
                a, b = ((first, second), (second, first))[h]
                width, at = ((CUT, 0), (WIDE - CUT, CUT))[h]
                for part in range(2):
                    source = stacks[(0 if h == owner else 2) + part]

                    def step(i, _):
                        block = me ^ ((i & 3) * z[0]) ^ ((i >> 2) * a[0]) ^ (part * b[0])
                        rows = pl.ds(pl.multiple_of(block * ROWS, 16), ROWS)
                        pltpu.make_async_copy(
                            source.at[i, :, 0:width], win.at[rows, at : at + width], sems.at[0]
                        ).start()
                        for r in range(2):
                            rows = pl.ds(pl.multiple_of((2 * block + r) * ROWS, 16), ROWS)
                            pltpu.make_async_copy(
                                source.at[i, :, OUT_AT[h] + r * half : OUT_AT[h] + (r + 1) * half],
                                wout.at[rows, h * half : (h + 1) * half],
                                sems.at[1],
                            ).start()
                        return 0

                    lax.fori_loop(0, BLOCKS // 2, step, 0)


def lane_of(value, h):
    turned = pltpu.roll(value, lax.rem(LANES - h, LANES), 1)
    return jnp.broadcast_to(turned[:, 0:1], value.shape)


def row_of(ref, h):
    return jnp.broadcast_to(ref[pl.ds(h, 1), :], (LANES, LANES))


class Setting:
    def __init__(self, ids, lens, small, section):
        self.small, self.section = small, section
        row = lax.broadcasted_iota(jnp.int32, (GROUP, LANES), 0)
        lane = lax.broadcasted_iota(jnp.int32, (GROUP, LANES), 1)
        self.lane = lane
        ends, total = [], 0
        for n in range(lens.shape[1]):
            total = total + lens[ids[1], n]
            ends.append(total)
        seg = lambda at: sum((at >= end).astype(jnp.int32) for end in ends)
        self.seg_row = seg(row)
        self.allowed = (self.seg_row == seg(lane)) & (row >= lane)
        self.keep = [
            ((seg(row - s) == self.seg_row) & (row >= s)).astype(f32) for s in range(1, CONV)
        ]
        self.lower = (row >= lane).astype(f32)
        self.upper = (row <= lane).astype(f32)

    def part(self, at, size=LANES):
        return self.small[self.section : self.section + 1, pl.ds(at, size)]

    def part_at(self, at, j):
        return self.small[self.section : self.section + 1, pl.ds(pl.multiple_of(at + j * LANES, LANES), LANES)]


def decay_parts(setting, proj, cum_ref, cum_t, step_ref, step_t):
    shifted = proj[:, RAW_AT : RAW_AT + LANES] + setting.part(STEP_AT)
    step = jnp.maximum(shifted, 0.0) + jnp.log1p(jnp.exp(-jnp.abs(shifted)))
    rate = -jnp.exp(setting.part(DECAY_AT))
    cum = exact_dot(setting.lower, step * rate)
    cum_ref[...] = cum
    step_ref[...] = step
    cum_t[...] = cum.T
    step_t[...] = step.T
    return shifted, rate


def state_parts(pre):
    keys = pre[:, INNER : INNER + STATE]
    queries = pre[:, INNER + STATE : INNER + 2 * STATE]
    return keys * sigmoid(keys), queries * sigmoid(queries)


def forward_block(setting, resid, wait_in, wait_out, win, wout, normed, proj, pre, scan, mixed, stat, out, tmp):
    cum_ref, cum_t, step_ref, step_t, gated_ref, kq_ref = tmp
    scale = lax.rsqrt(jnp.mean(resid * resid, axis=-1, keepdims=True) + eps_value)
    normed[...] = (resid * scale * setting.part(GAIN_AT, D)).astype(bf16)
    wait_in()
    for at in range(0, WIDE, 384):
        proj[:, at : at + 384] = jnp.dot(normed[...], win[:, at : at + 384], preferred_element_type=f32)

    def filter_step(j, _):
        x = proj[:, pl.ds(pl.multiple_of(INNER + j * LANES, LANES), LANES)]
        total = setting.part_at(SHIFT_AT, j) + x * setting.part_at(TAPS_AT + (CONV - 1) * CONV_CH, j)
        for s in range(1, CONV):
            tap = setting.part_at(TAPS_AT + (CONV - 1 - s) * CONV_CH, j)
            total = total + pltpu.roll(x, s, 0) * setting.keep[s - 1] * tap
        pre[:, chunk(j)] = total
        return 0

    lax.fori_loop(0, CONV_CH // LANES, filter_step, 0)
    decay_parts(setting, proj, cum_ref, cum_t, step_ref, step_t)
    keys, queries = state_parts(pre)
    kq_ref[...] = jnp.where(setting.allowed, exact_dot(queries, keys, nt_dims), 0.0)
    left = setting.lane < HEAD

    def pair_step(i, squares):
        v = pre[:, chunk(i)]
        v = v * sigmoid(v)
        mats = []
        for n in range(2):
            h = 2 * i + n
            spread = jnp.minimum(lane_of(cum_ref[...], h) - row_of(cum_t, h), 0.0)
            mats.append((jnp.exp(spread) * kq_ref[...] * row_of(step_t, h)).astype(bf16))
        vb = v.astype(bf16)
        zero = jnp.zeros_like(vb)
        stacked = jnp.concatenate([jnp.where(left, vb, zero), jnp.where(left, zero, vb)], 0)
        y = jnp.dot(jnp.concatenate(mats, 1), stacked, preferred_element_type=f32)
        skip = setting.part(SKIP_AT)
        skip = jnp.where(left[:1], lane_of(skip, 2 * i), lane_of(skip, 2 * i + 1))
        y = y + skip * v
        scan[:, chunk(i)] = y
        gate = proj[:, chunk(i)]
        gated = y * (gate * sigmoid(gate))
        gated_ref[:, chunk(i)] = gated
        return squares + gated * gated

    squares = lax.fori_loop(0, PAIRS, pair_step, jnp.zeros((GROUP, LANES), f32))
    mix = lax.rsqrt(jnp.sum(squares, axis=-1, keepdims=True) / INNER + eps_value)
    stat[...] = jnp.broadcast_to(mix, stat.shape)

    def mix_step(i, _):
        mixed[:, chunk(i)] = (gated_ref[:, chunk(i)] * stat[...] * setting.part_at(MIX_AT, i)).astype(bf16)
        return 0

    lax.fori_loop(0, PAIRS, mix_step, 0)
    wait_out()
    for at in range(0, D, 384):
        out[:, at : at + 384] = (
            resid[:, at : at + 384] + jnp.dot(mixed[...], wout[:, at : at + 384], preferred_element_type=f32)
        ).astype(bf16)


def backward_block(
    setting, resid, grad, wait_in, wait_out, win, wout, normed, proj, pre, scan, mixed, stat,
    grad_resid, grad_small, packs, tmp, more,
):
    cum_ref, cum_t, step_ref, step_t, dmix_ref, kq_ref = tmp
    dproj, dfilt, dkq_ref, rows_ref, cols_t = more
    shifted, rate = decay_parts(setting, proj, cum_ref, cum_t, step_ref, step_t)
    keys, queries = state_parts(pre)
    kq_ref[...] = jnp.where(setting.allowed, exact_dot(queries, keys, nt_dims), 0.0)
    left = setting.lane < HEAD
    down = lambda v: jnp.sum(v, axis=0, keepdims=True)
    wait_out()
    for at in range(0, INNER, 384):
        dmix_ref[:, at : at + 384] = lax.dot_general(
            grad[...], wout[at : at + 384, :], nt_dims, preferred_element_type=f32
        )
    turned = mixed[...].astype(f32).T.astype(bf16)
    part = jnp.dot(turned, grad[...], preferred_element_type=f32).astype(bf16).reshape(BLOCKS, 2, ROWS, D)
    half = D // 2
    for h in range(2):
        for r in range(2):
            at = OUT_AT[h] + r * half
            packs[h, :, :, at : at + half] = part[:, r, :, h * half : (h + 1) * half]
    packs[0, :, :, CUT + D : PACK] = jnp.zeros((BLOCKS, ROWS, PACK - CUT - D), bf16)

    def norm_step(i, total):
        gate = proj[:, chunk(i)]
        gated = scan[:, chunk(i)] * (gate * sigmoid(gate))
        dmix = dmix_ref[:, chunk(i)]
        grad_small[0:1, pl.ds(pl.multiple_of(MIX_AT + i * LANES, LANES), LANES)] = down(dmix * gated * stat[...])
        return total + dmix * setting.part_at(MIX_AT, i) * gated

    total = lax.fori_loop(0, PAIRS, norm_step, jnp.zeros((GROUP, LANES), f32))
    mix = stat[...]
    pull = mix * mix * mix * (jnp.sum(total, axis=-1, keepdims=True) / INNER)
    dkq_ref[...] = jnp.zeros_like(dkq_ref)
    rows_ref[...] = jnp.zeros_like(rows_ref)
    cols_t[...] = jnp.zeros_like(cols_t)

    def pair_step(i, skips):
        gate = proj[:, chunk(i)]
        gate_sig = sigmoid(gate)
        opened = gate * gate_sig
        y = scan[:, chunk(i)]
        dgated = stat[...] * (dmix_ref[:, chunk(i)] * setting.part_at(MIX_AT, i)) - y * opened * pull
        dproj[:, chunk(i)] = (dgated * y * (gate_sig * (1.0 + gate * (1.0 - gate_sig)))).astype(bf16)
        dy = dgated * opened
        v = pre[:, chunk(i)]
        v = v * sigmoid(v)
        skip = setting.part(SKIP_AT)
        skip = jnp.where(left[:1], lane_of(skip, 2 * i), lane_of(skip, 2 * i + 1))
        direct = down(dy * v)
        both_skips = (
            jnp.sum(jnp.where(left[:1], direct, 0.0), axis=1, keepdims=True),
            jnp.sum(jnp.where(left[:1], 0.0, direct), axis=1, keepdims=True),
        )
        split = lambda w: jnp.concatenate([jnp.where(left, w, jnp.zeros_like(w)), jnp.where(left, jnp.zeros_like(w), w)], 0)
        dyb, vb = dy.astype(bf16), v.astype(bf16)
        dmats = lax.dot_general(dyb, split(vb), nt_dims, preferred_element_type=f32)
        mats = []
        dkq = dkq_ref[...]
        row_sums = rows_ref[...]
        for n in range(2):
            h = 2 * i + n
            spread = jnp.minimum(lane_of(cum_ref[...], h) - row_of(cum_t, h), 0.0)
            decay = jnp.exp(spread)
            step_row = row_of(step_t, h)
            dmat = dmats[:, n * LANES : (n + 1) * LANES]
            bare = decay * kq_ref[...]
            mats.append((bare * step_row).T.astype(bf16))
            dkq = dkq + dmat * decay * step_row
            flow = dmat * bare
            cols_t[pl.ds(h, 1), :] = down(flow)
            row_sums = row_sums + jnp.where(
                setting.lane == h, jnp.sum(flow * step_row, axis=1, keepdims=True), 0.0
            )
            skips = skips + jnp.where(setting.lane[:1] == h, both_skips[n], 0.0)
        dkq_ref[...] = dkq
        rows_ref[...] = row_sums
        dv = jnp.dot(jnp.concatenate(mats, 1), split(dyb), preferred_element_type=f32)
        dfilt[:, chunk(i)] = dv + skip * dy
        return skips

    skips = lax.fori_loop(0, PAIRS, pair_step, jnp.zeros((1, LANES), f32))
    grad_small[0:1, SKIP_AT : SKIP_AT + LANES] = skips
    dkq = jnp.where(setting.allowed, dkq_ref[...], 0.0)
    dfilt[:, INNER : INNER + STATE] = exact_dot(dkq.T, queries)
    dfilt[:, INNER + STATE : CONV_CH] = exact_dot(dkq, keys)
    cols = cols_t[...].T
    after = exact_dot(setting.upper, rows_ref[...] - step_ref[...] * cols)
    draw = jnp.where(setting.lane < HEADS, (cols + rate * after) * sigmoid(shifted), 0.0)
    grad_small[0:1, STEP_AT : STEP_AT + LANES] = down(draw)
    grad_small[0:1, DECAY_AT : DECAY_AT + LANES] = down(after * step_ref[...] * rate)
    dproj[:, RAW_AT : RAW_AT + LANES] = draw.astype(bf16)

    def filter_step(j, _):
        x_at = pl.ds(pl.multiple_of(INNER + j * LANES, LANES), LANES)
        x = proj[:, x_at]
        p = pre[:, chunk(j)]
        sig = sigmoid(p)
        dpre = dfilt[:, chunk(j)] * (sig * (1.0 + p * (1.0 - sig)))
        put = lambda at, v: grad_small.__setitem__(
            (slice(0, 1), pl.ds(pl.multiple_of(at + j * LANES, LANES), LANES)), v
        )
        put(SHIFT_AT, down(dpre))
        put(TAPS_AT + (CONV - 1) * CONV_CH, down(dpre * x))
        dx = dpre * setting.part_at(TAPS_AT + (CONV - 1) * CONV_CH, j)
        for s in range(1, CONV):
            at = TAPS_AT + (CONV - 1 - s) * CONV_CH
            held = dpre * setting.keep[s - 1]
            put(at, down(held * pltpu.roll(x, s, 0)))
            dx = dx + pltpu.roll(held, GROUP - s, 0) * setting.part_at(at, j)
        dproj[:, x_at] = dx.astype(bf16)
        return 0

    lax.fori_loop(0, CONV_CH // LANES, filter_step, 0)
    turned = normed[...].astype(f32).T.astype(bf16)
    for h, (begin, end) in enumerate(((0, CUT), (CUT, WIDE))):
        for at in range(begin, end, 512):
            stop = min(at + 512, end)
            packs[h, :, :, at - begin : stop - begin] = (
                jnp.dot(turned, dproj[:, at:stop], preferred_element_type=f32)
                .astype(bf16)
                .reshape(BLOCKS, ROWS, stop - at)
            )
    wait_in()
    dnormed = lax.dot_general(dproj[...], win[...], nt_dims, preferred_element_type=f32)
    scale = lax.rsqrt(jnp.mean(resid * resid, axis=-1, keepdims=True) + eps_value)
    grad_small[0:1, GAIN_AT : GAIN_AT + D] = down(dnormed * resid * scale)
    pulled = dnormed * setting.part(GAIN_AT, D)
    inner = jnp.mean(pulled * resid, axis=-1, keepdims=True)
    grad_resid[...] = (
        grad[...].astype(f32) + scale * pulled - resid * (scale * scale * scale * inner)
    ).astype(bf16)


def send_packs(digits, ids, packs, kept, sent, sem):
    z, first, second = digits
    me, core = ids[0], ids[1]
    for owner in range(2):

        @pl.when(core == owner)
        def _():
            for h in range(2):
                a, b = ((first, second), (second, first))[h]
                target = kept if h == owner else sent
                for part in range(2):

                    def step(i, _):
                        block = me ^ ((i & 3) * z[0]) ^ ((i >> 2) * a[0]) ^ (part * b[0])
                        pltpu.make_async_copy(
                            packs.at[h, block], target.at[part * (BLOCKS // 2) + i], sem
                        ).start()
                        return 0

                    lax.fori_loop(0, BLOCKS // 2, step, 0)
    pltpu.make_async_copy(packs, packs, sem).wait()


KEPT = (
    ((GROUP, D), bf16),
    ((GROUP, WIDE), f32),
    ((GROUP, CONV_CH), f32),
    ((GROUP, INNER), f32),
    ((GROUP, INNER), bf16),
    ((GROUP, LANES), f32),
)
SQUARE = pltpu.VMEM((LANES, LANES), f32)
WEIGHTS = [pltpu.VMEM((D, WIDE), bf16), pltpu.VMEM((INNER, D), bf16), pltpu.SemaphoreType.DMA((2,))]
TMP = [SQUARE] * 4 + [pltpu.VMEM((GROUP, INNER), f32), SQUARE]
MORE = [pltpu.VMEM((GROUP, WIDE), bf16), pltpu.VMEM((GROUP, CONV_CH), f32), SQUARE, SQUARE, SQUARE]
PACKS = [pltpu.VMEM((2, BLOCKS, ROWS, PACK), bf16), pltpu.SemaphoreType.DMA]


def run_block(digits, section, passes, ids, lens, small, stacks, resid, grad=None, kept=()):
    forward, backward = "f" in passes, "b" in passes

    def kernel(*refs):
        refs = list(refs)
        take = lambda n: [refs.pop(0) for _ in range(n)]
        ids, lens, small = take(3)
        stacks = take(4)
        (resid_ref,) = take(1)
        grad_ref = take(1)[0] if backward else None
        held = take(len(KEPT)) if backward and not forward else None
        out = take(1)[0] if forward else None
        if forward and not backward:
            held = take(len(KEPT))
        if backward:
            grad_resid, grad_small, kept_out, sent_out = take(4)
        if forward and backward:
            held = take(len(KEPT))
        win, wout, sems = take(3)
        tmp = take(len(TMP))
        start_weights(digits, ids, stacks, win, wout, sems)
        setting = Setting(ids, lens, small, section)
        waited = set()

        def wait(ref, n):
            if n not in waited:
                waited.add(n)
                pltpu.make_async_copy(ref, ref, sems.at[n]).wait()

        waits = (lambda: wait(win, 0)), (lambda: wait(wout, 1))
        resid = resid_ref[...].astype(f32)
        if forward:
            forward_block(setting, resid, *waits, win, wout, *held, out, tmp)
        if backward:
            more = take(len(MORE))
            packs, sem = take(2)
            backward_block(
                setting, resid, grad_ref, *waits, win, wout, *held, grad_resid, grad_small, packs, tmp, more
            )
            send_packs(digits, ids, packs, kept_out, sent_out, sem)

    shape = jax.ShapeDtypeStruct
    vmem, smem, hbm = (pl.BlockSpec(memory_space=m) for m in (pltpu.VMEM, pltpu.SMEM, pl.ANY))
    in_specs = [smem, smem, vmem] + [hbm] * 4 + [vmem] * (1 + backward + len(kept))
    outs, out_specs, scratch = [], [], []
    if forward:
        outs.append(shape((GROUP, D), bf16))
        if not backward:
            outs += [shape(*k) for k in KEPT]
    out_specs += [vmem] * len(outs)
    if backward:
        stack = shape((BLOCKS, ROWS, PACK), bf16)
        outs += [shape((GROUP, D), bf16), shape((1, SMALL_SIZE), f32), stack, stack]
        out_specs += [vmem, vmem, hbm, hbm]
        if forward:
            scratch += [pltpu.VMEM(*k) for k in KEPT]
    scratch += WEIGHTS + TMP
    if backward:
        scratch += MORE + PACKS
    return pl.pallas_call(
        kernel,
        out_shape=outs,
        in_specs=in_specs,
        out_specs=out_specs,
        scratch_shapes=scratch,
        name=f"block{section}{passes}",
        cost_estimate=pl.CostEstimate(flops=10**9 * (1 + 2 * backward), bytes_accessed=12 * 10**6, transcendentals=10**6),
    )(ids, lens, small, *stacks, resid, *([grad] if backward else []), *kept)


def pack_small(parts):
    row, at = [], 0
    for (begin, shape), part in zip(SMALL, parts):
        row += [jnp.zeros((begin - at,), part.dtype)] * (begin > at) + [part.reshape(-1)]
        at = begin + part.size
    return jnp.concatenate(row + [jnp.zeros((SMALL_SIZE - at,), parts[0].dtype)])


def place_small(shards, me):
    parts = []
    for (_, shape), shard in zip(SMALL, shards):
        if shape == shard.shape:
            parts.append(jnp.where(me == 0, shard, jnp.zeros_like(shard)))
        else:
            at = (0,) * (len(shape) - 1) + (me * shard.shape[-1],)
            parts.append(lax.dynamic_update_slice(jnp.zeros(shape, shard.dtype), shard, at))
    return pack_small(parts)


def on_device(digits, tokens, cotangent, lengths, norm_gain, in_weight, filter_weight, filter_bias,
              step_bias, decay_log, skip_gain, mix_gain, out_weight):
    core = lax.axis_index("section")
    me = lax.axis_index("dp")
    first_core = core == 0
    pick = lambda a, b: jnp.where(first_core, a, b)
    shards = tuple(a[0] for a in (norm_gain, filter_weight, filter_bias, mix_gain, step_bias, decay_log, skip_gain))
    stacks = []
    if digits:
        first, second = pack_halves(in_weight[0], out_weight[0])
        other = swap_core(pick(second, first))
        for start in (pick(first, other), pick(other, second)):
            mine = gather_half(start, digits)
            stacks.append([*mine, *(swap_core(part) for part in mine)])
        own_small = place_small(shards, me)
        zero = jnp.zeros_like(own_small)
        small = sum_all(jnp.stack([pick(own_small, zero), pick(zero, own_small)]), digits)
        layout, ids = digits, jnp.stack([me, core])
    else:
        layout, ids = ((4, 4), (1, 2), (2, 2)), jnp.stack([0 * me, core])
        gather = lambda a, axis: lax.all_gather(
            lax.all_gather(a, "dp", axis=axis, tiled=True), "section", axis=0, tiled=True
        )
        in_all, out_all = gather(in_weight, 1), gather(out_weight, 1)
        for s in range(2):
            halves = pack_halves(in_all[s].reshape(BLOCKS, ROWS, PROJ), out_all[s].reshape(BLOCKS, 2 * ROWS, D))
            halves = [half[jnp.array(masks_of(layout)[h])] for h, half in enumerate(halves)]
            mine, theirs = pick(*halves), pick(*halves[::-1])
            stacks.append([mine[:8], mine[8:], theirs[:8], theirs[8:]])
        parts = (gather(norm_gain, 1), gather(filter_weight, 2), gather(filter_bias, 1), gather(mix_gain, 1)) + tuple(
            lax.all_gather(a, "section", axis=0, tiled=True) for a in (step_bias, decay_log, skip_gain)
        )
        small = jnp.stack([pack_small([part[s] for part in parts]) for s in range(2)])

    small = small.astype(f32)
    rows = lambda a: lax.dynamic_slice_in_dim(a, core * GROUP, GROUP, 0)
    start = rows(tokens)
    run = functools.partial(run_block, layout)
    middle, *kept = run(0, "f", ids, lengths[0], small, stacks[0], start)
    final, grad_1, small_1, kept_1, sent_1 = run(1, "fb", ids, lengths[0], small, stacks[1], middle, rows(cotangent))
    grad_0, small_0, kept_0, sent_0 = run(0, "b", ids, lengths[0], small, stacks[0], start, grad_1, kept)

    def own_rows(for_0, for_1):
        other = swap_core(pick(for_1, for_0))
        own = pick(for_0, for_1)
        return jnp.concatenate([pick(own, other), pick(other, own)])[None]

    section_outputs = own_rows(middle, final)
    input_grads = own_rows(grad_0, grad_1)
    small_sum = jnp.concatenate([small_0, small_1])
    if digits:
        done_1 = scatter_half(kept_1, sent_1, digits)
        done_0 = scatter_half(kept_0, sent_0, digits)
        other = swap_core(pick(done_1, done_0))
        own = pick(done_0, done_1)
        in_own, out_own = unpack_halves(pick(own, other), pick(other, own))
        small_sum = sum_all(small_sum, digits)
    else:
        ins, outs = [], []
        for mine, theirs in ((kept_0, sent_0), (kept_1, sent_1)):
            halves = [
                half[jnp.array([masks_of(layout)[h].index(b) for b in range(BLOCKS)])].astype(f32)
                for h, half in enumerate((pick(mine, theirs), pick(theirs, mine)))
            ]
            in_full, out_full = unpack_halves(*halves)
            ins.append(in_full.reshape(D, PROJ))
            outs.append(out_full.reshape(INNER, D))
        scatter = lambda a: lax.psum_scatter(
            lax.psum_scatter(a, "section", scatter_dimension=0, tiled=True), "dp", scatter_dimension=1, tiled=True)[0]
        in_own, out_own = scatter(jnp.stack(ins)), scatter(jnp.stack(outs))
        small_sum = lax.psum(small_sum, both)
    small_own = lax.dynamic_index_in_dim(small_sum, core, 0, keepdims=False)
    cut = []
    for (at, shape), shard in zip(SMALL, shards):
        size = 1
        for dim in shape:
            size *= dim
        part = small_own[at : at + size].reshape(shape)
        if shard.shape != shape:
            part = lax.dynamic_slice_in_dim(part, me * shard.shape[-1], shard.shape[-1], part.ndim - 1)
        cut.append(part[None])
    return (section_outputs, input_grads, cut[0], in_own[None], cut[1], cut[2], cut[4], cut[5], cut[6], cut[3],
            out_own[None])


def solution(mesh):
    placed = (
        P("dp", None), P("dp", None), P("dp", None, None), P("section", "dp"), P("section", "dp", None),
        P("section", None, "dp"), P("section", "dp"), P("section", None), P("section", None), P("section", None),
        P("section", "dp"), P("section", "dp", None),
    )
    return jax.shard_map(
        functools.partial(on_device, dp_digits(mesh)),
        mesh=mesh,
        in_specs=placed,
        out_specs=(
            P("section", "dp", None), P("section", "dp", None), P("section", "dp"), P("section", "dp", None),
            P("section", None, "dp"), P("section", "dp"), P("section", None), P("section", None),
            P("section", None), P("section", "dp"), P("section", "dp", None),
        ),
        check_vma=False,
    )
```
